512 devices in a mesh: freq: 128 (over y_lo, x, z), row: 4 (over y_hi, core).
Axes of the slice: x: 4, y: 4 (y_hi: 2, y_lo: 2; y = y_hi * 2 + y_lo), z: 16, core: 2. Of those that a mesh axis runs over, the one named last changes fastest.
Arguments:
- operator: bfloat16 [128, 1024, 2, 1024], P('freq', 'row'), may hold values from -0.125 to 0.125
- recorded: bfloat16 [128, 1024, 2, 512], P('freq', 'row'), may hold values from -6 to 6
- filter_coefficients: float32 [3, 8, 1024], P(None, None, ('row', 'freq')), may hold values from -1.2 to 1.2
- tap_delays: int32 [8], replicated, may hold values from 0 to 63, as said below
Outputs:
- primaries: bfloat16 [1024, 512, 1024], P(('row', 'freq'))
The draws below stay inside these ranges and needn't reach their ends.
Inputs may be any that keep to these rules, and one draw needn't show every extreme that they name: `tap_delays`: the delays are not distinct in general; at least one tap has delay 64 - 1.
All inputs are finite; a program needn't handle non-finite values.
Results may differ from the reference program's by a relative error of at most 0.008.
Values may be sent and summed in bfloat16 or wider, within the bound.
No kernel may reach another device: no remote copies, remote signals or barrier semaphores. Data moves between devices by JAX's collectives and lax.ppermute only.
A program may use at most 64 MiB of HBM per device.

```python
import math
import jax
import jax.numpy as jnp
from jax import lax

NS = 1024
NC = 512
NT = 1024
TAPS = 8
MAXLAG = 64
NF = 128
N_ROW = 4


def draw_tap_delays(key, part):
    first_key, second_key = jax.random.split(jax.random.fold_in(key, 17))
    values = jax.random.randint(first_key, (TAPS,), 0, MAXLAG)
    position = jax.random.randint(second_key, (), 0, TAPS)
    return values.at[position].set(MAXLAG - 1).astype(jnp.int32)


def levels(key, extent, cuts, least, top_value):
    loudness, own = 1.0, jax.random.fold_in(key, 6)
    for dim, shards_of in cuts:
        draws = jnp.exp(jax.random.uniform(jax.random.fold_in(own, dim), (shards_of,), jnp.float32, least / len(cuts), top_value / len(cuts)))
        loudness = loudness * jnp.repeat(draws, extent[dim] // shards_of).reshape([-1 if axis == dim else 1 for axis in range(len(extent))])
    return loudness


def bell_draw(stream_key, shape, width, bound, pieces=(), held_as=jnp.bfloat16):
    array = width * jax.random.normal(stream_key, shape, jnp.float32)
    if pieces:
        array = array * levels(stream_key, shape, pieces, -0.22, 0.18)
    return jnp.clip(array, -bound, bound).astype(held_as)


def setup_inputs(seed: int = 0) -> dict:
    seeds = jax.random.split(jax.random.key(seed), 5)
    return {
        "operator": bell_draw(seeds[0], (NF, NS, 2, NS), (2 * NS) ** -0.5, 0.125, ((0, 128), (1, 4))),
        "recorded": bell_draw(seeds[1], (NF, NS, 2, NC), 1.0, 6.0, ((0, 128), (1, 4))),
        "filter_coefficients": bell_draw(seeds[2], (3, TAPS, NS), 0.2, 1.2, ((2, 512),), jnp.float32),
        "tap_delays": draw_tap_delays(jax.random.fold_in(seeds[4], 71), 0),
    }


shrink_level = 0.5

def inverse_lookup(harmonics, time_step_total):
    overtone_indices = (jnp.arange(harmonics) + 1).astype(jnp.int32)
    recording_epochs = jnp.arange(time_step_total).astype(jnp.int32)
    rotation_radians = (overtone_indices[:, None] * recording_epochs[None, :] % time_step_total).astype(jnp.float32) * (2.0 * math.pi / time_step_total)
    scale = 1.0 / math.sqrt(harmonics)
    return jnp.stack([jnp.cos(rotation_radians) * scale, -jnp.sin(rotation_radians) * scale], axis=1).astype(jnp.bfloat16)

def complex_block(columns, segment):
    real_component = segment[:, 0]
    imag_part = segment[:, 1]
    upper = jnp.concatenate([real_component, imag_part], axis=1)
    lower = jnp.concatenate([-imag_part, real_component], axis=1)
    return jnp.dot(columns, jnp.concatenate([upper, lower], axis=0), preferred_element_type=jnp.float32)

def match_filter(border_rows, weights, tap_delays, row_count, time_step_total):
    padded = jnp.pad(border_rows, ((0, 0), (0, 0), (MAXLAG, 0)))
    estimate = jnp.zeros((row_count, border_rows.shape[1], time_step_total), jnp.float32)
    anchor = jnp.zeros((), jnp.int32)
    for tap_index in range(weights.shape[1]):
        begin = (MAXLAG - tap_delays[tap_index]).astype(jnp.int32)
        displaced_trace = lax.dynamic_slice(padded, (anchor, anchor, begin), (padded.shape[0], padded.shape[1], time_step_total))
        for neighbour in range(3):
            factor = weights[neighbour, tap_index][:, None, None]
            estimate = estimate + factor * displaced_trace[neighbour:neighbour + row_count].astype(jnp.float32)
    return estimate

def shrink(data_time, estimate):
    residual = data_time.astype(jnp.float32) - estimate
    return (jnp.sign(residual) * jnp.maximum(jnp.abs(residual) - shrink_level, 0.0)).astype(jnp.bfloat16)

def reference(operator, recorded, filter_coefficients, tap_delays):

    def one_frequency(pair):
        matrix, multiplicand = pair
        columns = matrix.reshape(NS, 2 * NS)
        return complex_block(columns, multiplicand).astype(jnp.bfloat16).reshape(NS, 2, NC)
    predicted = lax.map(one_frequency, (operator, recorded))
    table = inverse_lookup(NF, NT).astype(jnp.float32)
    line_rows = NS // N_ROW
    predicted_lines = jnp.moveaxis(predicted.reshape(NF, N_ROW, line_rows, 2, NC), 1, 0)
    recorded_lines = jnp.moveaxis(recorded.reshape(NF, N_ROW, line_rows, 2, NC), 1, 0)
    weight_lines = jnp.moveaxis(filter_coefficients.reshape(3, TAPS, N_ROW, line_rows), 2, 0)

    def one_line(triple):
        predicted_part, recorded_part, weight_part = triple
        multiples = jnp.einsum('frcs,fct->rst', predicted_part.astype(jnp.float32), table, precision=lax.Precision.HIGHEST).astype(jnp.bfloat16)
        data_time = jnp.einsum('frcs,fct->rst', recorded_part.astype(jnp.float32), table, precision=lax.Precision.HIGHEST).astype(jnp.bfloat16)
        border_rows = jnp.pad(multiples, ((1, 1), (0, 0), (0, 0)))
        estimate = match_filter(border_rows, weight_part, tap_delays, line_rows, NT)
        return shrink(data_time, estimate)
    primaries = lax.map(one_line, (predicted_lines, recorded_lines, weight_lines))
    return primaries.reshape(NS, NC, NT)
```

```python
import math

import jax
import jax.numpy as jnp
from jax import lax
from jax.sharding import PartitionSpec as P

NT = 1024
MAXLAG = 64
BLOCK = 128


shrink_level = 0.5


def inverse_lookup(harmonics, time_step_total):
    overtone_indices = jnp.arange(harmonics) + 1
    recording_epochs = jnp.arange(time_step_total)
    rotation_radians = (
        overtone_indices[:, None] * recording_epochs[None, :] % time_step_total
    ).astype(jnp.float32) * (2.0 * math.pi / time_step_total)
    scale = 1.0 / math.sqrt(harmonics)
    return jnp.stack(
        [jnp.cos(rotation_radians) * scale, -jnp.sin(rotation_radians) * scale], axis=1
    ).astype(jnp.bfloat16)


def filtered_tables(table, weights, tap_delays):
    harmonics = table.shape[0]
    neighbours, taps, stations = weights.shape
    kinds = neighbours * stations
    blocks = NT // BLOCK
    flat = jnp.pad(table.reshape(2 * harmonics, NT), ((0, 0), (MAXLAG, 0)))
    window = BLOCK + MAXLAG
    windows = jnp.stack(
        [flat[:, j * BLOCK : j * BLOCK + window] for j in range(blocks)], axis=1
    )
    lag = jnp.arange(BLOCK)[None, :] - jnp.arange(window)[:, None] + MAXLAG
    w = weights.transpose(1, 0, 2).reshape(taps, kinds)
    band = sum(
        w[k][None, :, None] * (lag == tap_delays[k]).astype(jnp.float32)[:, None, :]
        for k in range(taps)
    ).reshape(window, kinds * BLOCK)
    high = band.astype(jnp.bfloat16)
    low = (band - high.astype(jnp.float32)).astype(jnp.bfloat16)
    out = jnp.dot(
        jnp.concatenate([windows, windows], axis=2).reshape(-1, 2 * window),
        jnp.concatenate([high, low], axis=0),
        preferred_element_type=jnp.float32,
    ).astype(jnp.bfloat16)
    out = out.reshape(harmonics, 2, blocks, neighbours, stations, BLOCK)
    return out.transpose(3, 4, 0, 1, 2, 5).reshape(
        neighbours, stations, harmonics, 2, NT
    )


def body(operator, recorded, filter_coefficients, tap_delays):
    local_rows = operator.shape[1]
    freq_count = lax.axis_size("freq")
    row_count = lax.axis_size("row")
    row = lax.axis_index("row")

    def across(value, mask):
        return lax.ppermute(value, "row", [(i, i ^ mask) for i in range(row_count)])

    own = recorded[0]
    far = across(own, 2)
    recorded_traces = lax.all_to_all(
        recorded, "freq", split_axis=1, concat_axis=0, tiled=True
    )
    near = across(own, 1)
    far_near = across(far, 1)

    def complex_rows(mask):
        part = lax.dynamic_slice_in_dim(
            operator[0], (row ^ mask) * local_rows, local_rows, axis=2
        )
        real_part, imag_part = part[:, 0], part[:, 1]
        upper = jnp.stack([real_part, -imag_part], axis=-1)
        lower = jnp.stack([imag_part, real_part], axis=-1)
        return jnp.stack([upper, lower], axis=1)

    def product(mask, segment):
        return jnp.einsum(
            "rqsp,spc->rqc", complex_rows(mask), segment, preferred_element_type=jnp.float32
        )

    total = product(0, own) + product(1, near) + product(2, far) + product(3, far_near)
    spectra = total.astype(jnp.bfloat16)[None]
    traces = lax.all_to_all(spectra, "freq", split_axis=1, concat_axis=0, tiled=True)

    table = inverse_lookup(freq_count, NT)
    filter_coefficients, tap_delays, spectra = lax.optimization_barrier(
        (filter_coefficients, tap_delays, spectra)
    )
    filters = filtered_tables(table, filter_coefficients, tap_delays)

    def to_time(spectrum, basis):
        return jnp.einsum("fpc,fpt->ct", spectrum, basis, preferred_element_type=jnp.float32)

    forward = [(i, i + 1) for i in range(freq_count - 1)]
    backward = [(i + 1, i) for i in range(freq_count - 1)]
    before = lax.ppermute(traces[:, 1], "freq", forward)
    after = lax.ppermute(traces[:, 0], "freq", backward)
    data_time = [to_time(recorded_traces[:, s], table).astype(jnp.bfloat16) for s in range(2)]
    stations = [before, traces[:, 0], traces[:, 1], after]
    result = []
    for s in range(2):
        own_order = (1, 2, 0) if s == 0 else (0, 1, 2)
        estimate = sum(to_time(stations[s + n], filters[n, s]) for n in own_order)
        residual = data_time[s].astype(jnp.float32) - estimate
        result.append(
            (jnp.sign(residual) * jnp.maximum(jnp.abs(residual) - shrink_level, 0.0)).astype(
                jnp.bfloat16
            )
        )
    return jnp.stack(result)


def solution(mesh):
    in_specs = (
        P("freq", "row", None, None),
        P("freq", "row", None, None),
        P(None, None, ("row", "freq")),
        P(),
    )
    out_specs = P(("row", "freq"), None, None)
    return jax.shard_map(body, mesh=mesh, in_specs=in_specs, out_specs=out_specs, check_vma=False)
```

```python
import math

import jax
import jax.numpy as jnp
from jax import lax
from jax.experimental import pallas as pl
from jax.experimental.layout import Layout, with_layout_constraint
from jax.experimental.pallas import tpu as pltpu
from jax.sharding import PartitionSpec as P


NT = 1024
BLOCK = 128
COLUMNS = 256


shrink_level = 0.5


def lookup_rows(frequency_index):
    harmonics = frequency_index.shape[0]
    recording_epochs = jnp.arange(NT)
    rotation_radians = (
        frequency_index[:, None] * recording_epochs[None, :] % NT
    ).astype(jnp.float32) * (2.0 * math.pi / NT)
    scale = 1.0 / math.sqrt(harmonics)
    return jnp.stack(
        [jnp.cos(rotation_radians) * scale, -jnp.sin(rotation_radians) * scale], axis=1
    ).astype(jnp.bfloat16).reshape(2 * harmonics, NT)


def band_matrix(weights_ref, delays_ref, neighbour, station, first):
    taps = delays_ref.shape[0]
    shape = (2 * BLOCK, BLOCK)
    before = lax.broadcasted_iota(jnp.int32, shape, 0)
    lag = lax.broadcasted_iota(jnp.int32, shape, 1) - before + BLOCK
    band = jnp.zeros(shape, jnp.float32)
    for k in range(taps):
        weight = weights_ref[(neighbour * taps + k) * 2 + station]
        band += jnp.where(lag == delays_ref[k], weight, 0.0)
    band = jnp.where(first & (before < BLOCK), 0.0, band)
    high = band.astype(jnp.bfloat16)
    return high, (band - high.astype(jnp.float32)).astype(jnp.bfloat16)


def tables_kernel(weights_ref, delays_ref, last_ref, here_ref, out_ref):
    station = pl.program_id(0)
    first = pl.program_id(1) == 0
    rows = here_ref.shape[0]
    window = jnp.concatenate([last_ref[...], here_ref[...]], axis=1)
    for neighbour in range(3):
        parts = band_matrix(weights_ref, delays_ref, neighbour, station, first)
        filtered = sum(
            jnp.dot(window, part, preferred_element_type=jnp.float32) for part in parts
        )
        out_ref[0, pl.ds(neighbour * rows, rows)] = filtered.astype(jnp.bfloat16)


def filtered_tables(table, weights, tap_delays):
    rows = table.shape[0]
    return pl.pallas_call(
        tables_kernel,
        grid=(2, NT // BLOCK),
        out_shape=jax.ShapeDtypeStruct((2, 3 * rows, NT), jnp.bfloat16),
        in_specs=[
            pl.BlockSpec(memory_space=pltpu.SMEM),
            pl.BlockSpec(memory_space=pltpu.SMEM),
            pl.BlockSpec((rows, BLOCK), lambda s, b: (0, jnp.maximum(b - 1, 0))),
            pl.BlockSpec((rows, BLOCK), lambda s, b: (0, b)),
        ],
        out_specs=pl.BlockSpec((1, 3 * rows, BLOCK), lambda s, b: (s, 0, b)),
        cost_estimate=pl.CostEstimate(
            flops=48 * rows * NT * BLOCK, bytes_accessed=16 * rows * NT, transcendentals=0
        ),
        name="tables",
    )(weights.reshape(-1), tap_delays, table, table)


def across_time(spectrum, basis):
    return lax.dot_general(
        spectrum, basis, (((0,), (0,)), ((), ())), preferred_element_type=jnp.float32
    )


def data_kernel(recorded_ref, table_ref, out_ref):
    out_ref[0] = across_time(recorded_ref[0], table_ref[...]).astype(jnp.bfloat16)


def data_part(recorded, table):
    _, rows, columns = recorded.shape
    return pl.pallas_call(
        data_kernel,
        grid=(2, columns // COLUMNS),
        out_shape=jax.ShapeDtypeStruct((2, columns, NT), jnp.bfloat16),
        in_specs=[
            pl.BlockSpec((1, rows, COLUMNS), lambda s, c: (s, 0, c)),
            pl.BlockSpec((rows, NT), lambda s, c: (0, 0)),
        ],
        out_specs=pl.BlockSpec((1, COLUMNS, NT), lambda s, c: (s, c, 0)),
        cost_estimate=pl.CostEstimate(
            flops=4 * rows * columns * NT, bytes_accessed=6 * columns * NT, transcendentals=0
        ),
        name="data",
    )(recorded, table)


def final_kernel(before_ref, first_ref, second_ref, after_ref, basis_ref, data_ref, out_ref):
    station = pl.program_id(0)

    def finish(refs):
        spectra = jnp.concatenate([ref[...] for ref in refs], axis=0)
        residual = data_ref[0].astype(jnp.float32) - across_time(spectra, basis_ref[0])
        shrunk = residual - jnp.clip(residual, -shrink_level, shrink_level)
        out_ref[0] = shrunk.astype(jnp.bfloat16)

    @pl.when(station == 0)
    def _():
        finish([before_ref, first_ref, second_ref])

    @pl.when(station == 1)
    def _():
        finish([first_ref, second_ref, after_ref])


def final_part(before, first, second, after, basis, data):
    rows, columns = before.shape
    spectra = pl.BlockSpec((rows, COLUMNS), lambda s, c: (0, c))
    return pl.pallas_call(
        final_kernel,
        grid=(2, columns // COLUMNS),
        out_shape=jax.ShapeDtypeStruct((2, columns, NT), jnp.bfloat16),
        in_specs=[
            spectra,
            spectra,
            spectra,
            spectra,
            pl.BlockSpec((1, 3 * rows, NT), lambda s, c: (s, 0, 0)),
            pl.BlockSpec((1, COLUMNS, NT), lambda s, c: (s, c, 0)),
        ],
        out_specs=pl.BlockSpec((1, COLUMNS, NT), lambda s, c: (s, c, 0)),
        cost_estimate=pl.CostEstimate(
            flops=12 * rows * columns * NT, bytes_accessed=12 * columns * NT, transcendentals=0
        ),
        name="final",
    )(before, first, second, after, basis, data)


def body(operator, recorded, filter_coefficients, tap_delays):
    local_rows = operator.shape[1]
    columns = recorded.shape[3]
    freq_count = lax.axis_size("freq")
    row_count = lax.axis_size("row")
    row = lax.axis_index("row")

    plain = Layout(major_to_minor=(0, 1, 2, 3))

    def across(value, mask):
        pairs = [(i, i ^ mask) for i in range(row_count)]
        return with_layout_constraint(lax.ppermute(value, "row", pairs), plain)

    recorded_traces = lax.all_to_all(
        recorded, "freq", split_axis=1, concat_axis=0, tiled=True
    )
    far = across(recorded, 2)
    near = across(recorded, 1)
    far_near = across(far, 1)

    planes = lax.optimization_barrier(operator[0].transpose(1, 0, 2))

    def product(mask, segment):
        real_part, imag_part = lax.dynamic_slice_in_dim(
            planes, (row ^ mask) * local_rows, local_rows, axis=2
        )
        block = jnp.stack(
            [jnp.stack([real_part, -imag_part]), jnp.stack([imag_part, real_part])]
        )
        return jnp.einsum(
            "qprs,spc->rqc", block, segment[0], preferred_element_type=jnp.float32
        )

    total = product(0, recorded) + product(1, near)
    total = total + product(2, far) + product(3, far_near)
    spectra = total.astype(jnp.bfloat16)[None]
    traces = lax.all_to_all(spectra, "freq", split_axis=1, concat_axis=0, tiled=True)

    frequency_index, weights, _ = lax.optimization_barrier(
        (jnp.arange(freq_count) + 1, filter_coefficients, spectra)
    )
    table = lookup_rows(frequency_index)
    basis = filtered_tables(table, weights, tap_delays)

    def by_station(gathered):
        return [gathered[:, s].reshape(2 * freq_count, columns) for s in range(2)]

    recorded_traces = jnp.stack(by_station(recorded_traces))
    data = data_part(recorded_traces, table)

    forward = [(i, i + 1) for i in range(freq_count - 1)]
    backward = [(i + 1, i) for i in range(freq_count - 1)]
    first, second = by_station(traces)
    before = lax.ppermute(second, "freq", forward)
    after = lax.ppermute(first, "freq", backward)
    return final_part(before, first, second, after, basis, data)


def solution(mesh):
    in_specs = (
        P("freq", "row", None, None),
        P("freq", "row", None, None),
        P(None, None, ("row", "freq")),
        P(),
    )
    out_specs = P(("row", "freq"), None, None)


    return jax.shard_map(body, mesh=mesh, in_specs=in_specs, out_specs=out_specs, check_vma=False)
```

```python
import math

import jax
import jax.numpy as jnp
from jax import lax
from jax.experimental import pallas as pl
from jax.experimental.layout import Layout, with_layout_constraint
from jax.experimental.pallas import tpu as pltpu
from jax.sharding import PartitionSpec as P


NT = 1024
BLOCK = 128
COLUMNS = 256


shrink_level = 0.5


def lookup_rows(frequency_index):
    harmonics = frequency_index.shape[0]
    recording_epochs = jnp.arange(NT)
    rotation_radians = (
        frequency_index[:, None] * recording_epochs[None, :] % NT
    ).astype(jnp.float32) * (2.0 * math.pi / NT)
    scale = 1.0 / math.sqrt(harmonics)
    return jnp.stack(
        [jnp.cos(rotation_radians) * scale, -jnp.sin(rotation_radians) * scale], axis=1
    ).astype(jnp.bfloat16).reshape(2 * harmonics, NT)


def tables_kernel(weights_ref, delays_ref, last_ref, here_ref, out_ref, high_ref, low_ref):
    station = pl.program_id(0)
    first = pl.program_id(1) == 0
    rows = here_ref.shape[0]
    taps = delays_ref.shape[0]

    @pl.when(first)
    def _():
        shape = (2 * BLOCK, BLOCK)
        lag = (
            lax.broadcasted_iota(jnp.int32, shape, 1)
            - lax.broadcasted_iota(jnp.int32, shape, 0)
            + BLOCK
        )
        for part in range(3):
            neighbour = lax.rem(part + 1 - station, 3)
            band = jnp.zeros(shape, jnp.float32)
            for k in range(taps):
                weight = weights_ref[(neighbour * taps + k) * 2 + station]
                band += jnp.where(lag == delays_ref[k], weight, 0.0)
            high = band.astype(jnp.bfloat16)
            at = pl.ds(part * BLOCK, BLOCK)
            high_ref[:, at] = high
            low_ref[:, at] = (band - high.astype(jnp.float32)).astype(jnp.bfloat16)

    last = jnp.where(first, jnp.zeros_like(last_ref[...]), last_ref[...])
    window = jnp.concatenate([last, here_ref[...]], axis=1)
    filtered = jnp.dot(window, high_ref[...], preferred_element_type=jnp.float32)
    filtered += jnp.dot(window, low_ref[...], preferred_element_type=jnp.float32)
    for part in range(3):
        out_ref[0, pl.ds(part * rows, rows)] = filtered[
            :, part * BLOCK : (part + 1) * BLOCK
        ].astype(jnp.bfloat16)


def filtered_tables(table, weights, tap_delays):
    rows = table.shape[0]
    return pl.pallas_call(
        tables_kernel,
        grid=(2, NT // BLOCK),
        out_shape=jax.ShapeDtypeStruct((2, 3 * rows, NT), jnp.bfloat16),
        in_specs=[
            pl.BlockSpec(memory_space=pltpu.SMEM),
            pl.BlockSpec(memory_space=pltpu.SMEM),
            pl.BlockSpec((rows, BLOCK), lambda s, b: (0, jnp.maximum(b - 1, 0))),
            pl.BlockSpec((rows, BLOCK), lambda s, b: (0, b)),
        ],
        out_specs=pl.BlockSpec((1, 3 * rows, BLOCK), lambda s, b: (s, 0, b)),
        scratch_shapes=[pltpu.VMEM((2 * BLOCK, 3 * BLOCK), jnp.bfloat16)] * 2,
        cost_estimate=pl.CostEstimate(
            flops=48 * rows * NT * BLOCK, bytes_accessed=16 * rows * NT, transcendentals=0
        ),
        name="tables",
    )(weights.reshape(-1), tap_delays, table, table)


def across_time(spectrum, basis):
    return lax.dot_general(
        spectrum, basis, (((0,), (0,)), ((), ())), preferred_element_type=jnp.float32
    )


def data_kernel(recorded_ref, table_ref, out_ref):
    out_ref[0] = across_time(recorded_ref[0], table_ref[...]).astype(jnp.bfloat16)


def data_part(recorded, table):
    _, rows, columns = recorded.shape
    return pl.pallas_call(
        data_kernel,
        grid=(2, columns // COLUMNS),
        out_shape=jax.ShapeDtypeStruct((2, columns, NT), jnp.bfloat16),
        in_specs=[
            pl.BlockSpec((1, rows, COLUMNS), lambda s, c: (s, 0, c)),
            pl.BlockSpec((rows, NT), lambda s, c: (0, 0)),
        ],
        out_specs=pl.BlockSpec((1, COLUMNS, NT), lambda s, c: (s, c, 0)),
        cost_estimate=pl.CostEstimate(
            flops=4 * rows * columns * NT, bytes_accessed=6 * columns * NT, transcendentals=0
        ),
        name="data",
    )(recorded, table)


def own_kernel(first_ref, second_ref, basis_ref, data_ref, out_ref):
    spectra = jnp.concatenate([first_ref[...], second_ref[...]], axis=0)
    out_ref[0] = data_ref[0].astype(jnp.float32) - across_time(spectra, basis_ref[0])


def own_part(first, second, basis, data):
    rows, columns = first.shape
    spectra = pl.BlockSpec((rows, COLUMNS), lambda s, c: (0, c))
    return pl.pallas_call(
        own_kernel,
        grid=(2, columns // COLUMNS),
        out_shape=jax.ShapeDtypeStruct((2, columns, NT), jnp.float32),
        in_specs=[
            spectra,
            spectra,
            pl.BlockSpec((1, 2 * rows, NT), lambda s, c: (s, 0, 0)),
            pl.BlockSpec((1, COLUMNS, NT), lambda s, c: (s, c, 0)),
        ],
        out_specs=pl.BlockSpec((1, COLUMNS, NT), lambda s, c: (s, c, 0)),
        cost_estimate=pl.CostEstimate(
            flops=8 * rows * columns * NT, bytes_accessed=12 * columns * NT, transcendentals=0
        ),
        name="own",
    )(first, second, basis, data)


def final_kernel(before_ref, after_ref, basis_ref, rest_ref, out_ref):
    halo = jnp.where(pl.program_id(0) == 0, before_ref[...], after_ref[...])
    residual = rest_ref[0] - across_time(halo, basis_ref[0])
    shrunk = residual - jnp.clip(residual, -shrink_level, shrink_level)
    out_ref[0] = shrunk.astype(jnp.bfloat16)


def final_part(before, after, basis, rest):
    rows, columns = before.shape
    spectra = pl.BlockSpec((rows, COLUMNS), lambda s, c: (0, c))
    return pl.pallas_call(
        final_kernel,
        grid=(2, columns // COLUMNS),
        out_shape=jax.ShapeDtypeStruct((2, columns, NT), jnp.bfloat16),
        in_specs=[
            spectra,
            spectra,
            pl.BlockSpec((1, rows, NT), lambda s, c: (s, 2, 0)),
            pl.BlockSpec((1, COLUMNS, NT), lambda s, c: (s, c, 0)),
        ],
        out_specs=pl.BlockSpec((1, COLUMNS, NT), lambda s, c: (s, c, 0)),
        cost_estimate=pl.CostEstimate(
            flops=4 * rows * columns * NT, bytes_accessed=14 * columns * NT, transcendentals=0
        ),
        name="final",
    )(before, after, basis, rest)


def body(operator, recorded, filter_coefficients, tap_delays):
    local_rows = operator.shape[1]
    columns = recorded.shape[3]
    freq_count = lax.axis_size("freq")
    row_count = lax.axis_size("row")
    row = lax.axis_index("row")

    plain = Layout(major_to_minor=(0, 1, 2, 3))

    def across(value, mask):
        pairs = [(i, i ^ mask) for i in range(row_count)]
        return with_layout_constraint(lax.ppermute(value, "row", pairs), plain)

    recorded_traces = lax.all_to_all(
        recorded, "freq", split_axis=1, concat_axis=0, tiled=True
    )
    far = across(recorded, 2)
    near = across(recorded, 1)
    far_near = across(far, 1)

    planes = lax.optimization_barrier(operator[0].transpose(1, 0, 2))

    def product(mask, segment):
        real_part, imag_part = lax.dynamic_slice_in_dim(
            planes, (row ^ mask) * local_rows, local_rows, axis=2
        )
        block = jnp.stack(
            [jnp.stack([real_part, -imag_part]), jnp.stack([imag_part, real_part])]
        )
        return jnp.einsum(
            "qprs,spc->rqc", block, segment[0], preferred_element_type=jnp.float32
        )

    total = product(0, recorded) + product(1, near)
    total = total + product(2, far) + product(3, far_near)
    spectra = total.astype(jnp.bfloat16)[None]
    traces = lax.all_to_all(spectra, "freq", split_axis=1, concat_axis=0, tiled=True)

    table = lookup_rows(jnp.arange(freq_count) + 1)
    basis = filtered_tables(table, filter_coefficients, tap_delays)

    def by_station(gathered):
        return [gathered[:, s].reshape(2 * freq_count, columns) for s in range(2)]

    recorded_traces = jnp.stack(by_station(recorded_traces))
    data = data_part(recorded_traces, table)

    forward = [(i, i + 1) for i in range(freq_count - 1)]
    backward = [(i + 1, i) for i in range(freq_count - 1)]
    first, second = by_station(traces)
    before = lax.ppermute(second, "freq", forward)
    after = lax.ppermute(first, "freq", backward)
    rest = own_part(first, second, basis, data)
    return final_part(before, after, basis, rest)


def solution(mesh):
    in_specs = (
        P("freq", "row", None, None),
        P("freq", "row", None, None),
        P(None, None, ("row", "freq")),
        P(),
    )
    out_specs = P(("row", "freq"), None, None)


    return jax.shard_map(body, mesh=mesh, in_specs=in_specs, out_specs=out_specs, check_vma=False)
```

```python
import math

import jax
import jax.numpy as jnp
from jax import lax
from jax.experimental import pallas as pl
from jax.experimental.layout import Layout, with_layout_constraint
from jax.experimental.pallas import tpu as pltpu
from jax.sharding import PartitionSpec as P


NT = 1024
BLOCK = 128


shrink_level = 0.5


def lookup_rows(frequency_index):
    harmonics = frequency_index.shape[0]
    recording_epochs = jnp.arange(NT)
    rotation_radians = (
        frequency_index[:, None] * recording_epochs[None, :] % NT
    ).astype(jnp.float32) * (2.0 * math.pi / NT)
    scale = 1.0 / math.sqrt(harmonics)
    return jnp.stack(
        [jnp.cos(rotation_radians) * scale, -jnp.sin(rotation_radians) * scale], axis=1
    ).astype(jnp.bfloat16).reshape(2 * harmonics, NT)


def tables_kernel(weights_ref, delays_ref, last_ref, here_ref, out_ref, high_ref, low_ref):
    station = pl.program_id(0)
    first = pl.program_id(1) == 0
    rows = here_ref.shape[0]
    taps = delays_ref.shape[0]

    @pl.when(first)
    def _():
        shape = (2 * BLOCK, BLOCK)
        lag = (
            lax.broadcasted_iota(jnp.int32, shape, 1)
            - lax.broadcasted_iota(jnp.int32, shape, 0)
            + BLOCK
        )
        for part in range(3):
            neighbour = lax.rem(part + 1 - station, 3)
            band = jnp.zeros(shape, jnp.float32)
            for k in range(taps):
                weight = weights_ref[(neighbour * taps + k) * 2 + station]
                band += jnp.where(lag == delays_ref[k], weight, 0.0)
            high = band.astype(jnp.bfloat16)
            at = pl.ds(part * BLOCK, BLOCK)
            high_ref[:, at] = high
            low_ref[:, at] = (band - high.astype(jnp.float32)).astype(jnp.bfloat16)

    last = jnp.where(first, jnp.zeros_like(last_ref[...]), last_ref[...])
    window = jnp.concatenate([last, here_ref[...]], axis=1)
    filtered = jnp.dot(window, high_ref[...], preferred_element_type=jnp.float32)
    filtered += jnp.dot(window, low_ref[...], preferred_element_type=jnp.float32)
    for part in range(3):
        out_ref[0, pl.ds(part * rows, rows)] = filtered[
            :, part * BLOCK : (part + 1) * BLOCK
        ].astype(jnp.bfloat16)


def filtered_tables(table, weights, tap_delays):
    rows = table.shape[0]
    return pl.pallas_call(
        tables_kernel,
        grid=(2, NT // BLOCK),
        out_shape=jax.ShapeDtypeStruct((2, 3 * rows, NT), jnp.bfloat16),
        in_specs=[
            pl.BlockSpec(memory_space=pltpu.SMEM),
            pl.BlockSpec(memory_space=pltpu.SMEM),
            pl.BlockSpec((rows, BLOCK), lambda s, b: (0, jnp.maximum(b - 1, 0))),
            pl.BlockSpec((rows, BLOCK), lambda s, b: (0, b)),
        ],
        out_specs=pl.BlockSpec((1, 3 * rows, BLOCK), lambda s, b: (s, 0, b)),
        scratch_shapes=[pltpu.VMEM((2 * BLOCK, 3 * BLOCK), jnp.bfloat16)] * 2,
        cost_estimate=pl.CostEstimate(
            flops=48 * rows * NT * BLOCK, bytes_accessed=16 * rows * NT, transcendentals=0
        ),
        name="tables",
    )(weights.reshape(-1), tap_delays, table, table)


def body(operator, recorded, filter_coefficients, tap_delays):
    local_rows = operator.shape[1]
    columns = recorded.shape[3]
    freq_count = lax.axis_size("freq")
    row_count = lax.axis_size("row")
    row = lax.axis_index("row")

    plain = Layout(major_to_minor=(0, 1, 2, 3))

    def across(value, mask):
        pairs = [(i, i ^ mask) for i in range(row_count)]
        return with_layout_constraint(lax.ppermute(value, "row", pairs), plain)

    recorded_traces = lax.all_to_all(
        recorded, "freq", split_axis=1, concat_axis=0, tiled=True
    )
    far = across(recorded, 2)
    near = across(recorded, 1)
    far_near = across(far, 1)

    planes = lax.optimization_barrier(operator[0].transpose(1, 0, 2))

    def product(mask, segment):
        real_part, imag_part = lax.dynamic_slice_in_dim(
            planes, (row ^ mask) * local_rows, local_rows, axis=2
        )
        block = jnp.stack(
            [jnp.stack([real_part, -imag_part]), jnp.stack([imag_part, real_part])]
        )
        return jnp.einsum(
            "qprs,spc->rqc", block, segment[0], preferred_element_type=jnp.float32
        )

    total = product(0, recorded) + product(1, near)
    total = total + product(2, far) + product(3, far_near)
    spectra = total.astype(jnp.bfloat16)[None]
    traces = lax.all_to_all(spectra, "freq", split_axis=1, concat_axis=0, tiled=True)

    frequency_index, weights, _ = lax.optimization_barrier(
        (jnp.arange(freq_count) + 1, filter_coefficients, spectra)
    )
    table = lookup_rows(frequency_index)
    basis = filtered_tables(table, weights, tap_delays)

    def station_rows(gathered, s):
        return gathered[:, s].reshape(2 * freq_count, columns)

    def turned(spectra):
        return with_layout_constraint(spectra.T, Layout(major_to_minor=(0, 1)))

    def to_time(spectra, basis):
        return with_layout_constraint(
            jnp.dot(spectra, basis, preferred_element_type=jnp.float32),
            Layout(major_to_minor=(0, 1)),
        )

    rows = 2 * freq_count
    data = [
        to_time(turned(station_rows(recorded_traces, s)), table).astype(jnp.bfloat16)
        for s in range(2)
    ]

    forward = [(i, i + 1) for i in range(freq_count - 1)]
    backward = [(i + 1, i) for i in range(freq_count - 1)]
    first, second = station_rows(traces, 0), station_rows(traces, 1)
    before = lax.ppermute(second, "freq", forward)
    after = lax.ppermute(first, "freq", backward)
    own = turned(jnp.concatenate([first, second], axis=0))
    rest = [
        data[s].astype(jnp.float32) - to_time(own, basis[s, : 2 * rows]) for s in range(2)
    ]
    result = []
    for s, halo in enumerate((before, after)):
        residual = rest[s] - to_time(turned(halo), basis[s, 2 * rows :])
        shrunk = residual - jnp.clip(residual, -shrink_level, shrink_level)
        result.append(shrunk.astype(jnp.bfloat16))
    return jnp.stack(result)


def solution(mesh):
    in_specs = (
        P("freq", "row", None, None),
        P("freq", "row", None, None),
        P(None, None, ("row", "freq")),
        P(),
    )
    out_specs = P(("row", "freq"), None, None)


    return jax.shard_map(body, mesh=mesh, in_specs=in_specs, out_specs=out_specs, check_vma=False)
```

```python
import math

import jax
import jax.numpy as jnp
from jax import lax
from jax.experimental import pallas as pl
from jax.experimental.layout import Layout, with_layout_constraint
from jax.experimental.pallas import tpu as pltpu
from jax.sharding import Mesh
from jax.sharding import PartitionSpec as P


NT = 1024
BLOCK = 128
FREQ = ("yl", "x", "z")
ROW = ("yh", "core")
SIZES = (2, 4, 16, 2, 2)


shrink_level = 0.5


def lookup_rows(frequency_index):
    harmonics = frequency_index.shape[0]
    recording_epochs = jnp.arange(NT)
    rotation_radians = (
        frequency_index[:, None] * recording_epochs[None, :] % NT
    ).astype(jnp.float32) * (2.0 * math.pi / NT)
    scale = 1.0 / math.sqrt(harmonics)
    return jnp.stack(
        [jnp.cos(rotation_radians) * scale, -jnp.sin(rotation_radians) * scale], axis=1
    ).astype(jnp.bfloat16).reshape(2 * harmonics, NT)


def tables_kernel(weights_ref, delays_ref, last_ref, here_ref, out_ref, high_ref, low_ref):
    station = pl.program_id(0)
    first = pl.program_id(1) == 0
    rows = here_ref.shape[0]
    taps = delays_ref.shape[0]

    @pl.when(first)
    def _():
        shape = (2 * BLOCK, BLOCK)
        lag = (
            lax.broadcasted_iota(jnp.int32, shape, 1)
            - lax.broadcasted_iota(jnp.int32, shape, 0)
            + BLOCK
        )
        for part in range(3):
            neighbour = lax.rem(part + 1 - station, 3)
            band = jnp.zeros(shape, jnp.float32)
            for k in range(taps):
                weight = weights_ref[(neighbour * taps + k) * 2 + station]
                band += jnp.where(lag == delays_ref[k], weight, 0.0)
            high = band.astype(jnp.bfloat16)
            at = pl.ds(part * BLOCK, BLOCK)
            high_ref[:, at] = high
            low_ref[:, at] = (band - high.astype(jnp.float32)).astype(jnp.bfloat16)

    last = jnp.where(first, jnp.zeros_like(last_ref[...]), last_ref[...])
    window = jnp.concatenate([last, here_ref[...]], axis=1)
    filtered = jnp.dot(window, high_ref[...], preferred_element_type=jnp.float32)
    filtered += jnp.dot(window, low_ref[...], preferred_element_type=jnp.float32)
    for part in range(3):
        out_ref[0, pl.ds(part * rows, rows)] = filtered[
            :, part * BLOCK : (part + 1) * BLOCK
        ].astype(jnp.bfloat16)


def filtered_tables(table, weights, tap_delays):
    rows = table.shape[0]
    return pl.pallas_call(
        tables_kernel,
        grid=(2, NT // BLOCK),
        out_shape=jax.ShapeDtypeStruct((2, 3 * rows, NT), jnp.bfloat16),
        in_specs=[
            pl.BlockSpec(memory_space=pltpu.SMEM),
            pl.BlockSpec(memory_space=pltpu.SMEM),
            pl.BlockSpec((rows, BLOCK), lambda s, b: (0, jnp.maximum(b - 1, 0))),
            pl.BlockSpec((rows, BLOCK), lambda s, b: (0, b)),
        ],
        out_specs=pl.BlockSpec((1, 3 * rows, BLOCK), lambda s, b: (s, 0, b)),
        scratch_shapes=[pltpu.VMEM((2 * BLOCK, 3 * BLOCK), jnp.bfloat16)] * 2,
        cost_estimate=pl.CostEstimate(
            flops=48 * rows * NT * BLOCK, bytes_accessed=16 * rows * NT, transcendentals=0
        ),
        name="tables",
    )(weights.reshape(-1), tap_delays, table, table)


def body(operator, recorded, filter_coefficients, tap_delays):
    local_rows = operator.shape[1]
    columns = recorded.shape[3]
    freq_count = lax.axis_size(FREQ)
    row_count = lax.axis_size(ROW)
    row = lax.axis_index(ROW)

    plain = Layout(major_to_minor=(0, 1, 2, 3))

    def across(value, mask):
        pairs = [(i, i ^ mask) for i in range(row_count)]
        return with_layout_constraint(lax.ppermute(value, ROW, pairs), plain)

    spread, width, rungs = (lax.axis_size(axis) for axis in FREQ)
    spots = spread * width
    pairs = local_rows // freq_count

    by_target = recorded.reshape(spots, rungs, pairs, 2, columns).transpose(1, 0, 2, 3, 4)
    line = lax.all_to_all(by_target, "z", split_axis=0, concat_axis=0, tiled=True)

    far = across(recorded, 2)
    near = across(recorded, 1)
    far_near = across(far, 1)

    planes = lax.optimization_barrier(operator[0].transpose(1, 0, 2))

    def product(mask, segment):
        real_part, imag_part = lax.dynamic_slice_in_dim(
            planes, (row ^ mask) * local_rows, local_rows, axis=2
        )
        block = jnp.stack(
            [jnp.stack([real_part, -imag_part]), jnp.stack([imag_part, real_part])]
        )
        return jnp.einsum(
            "qprs,spc->rqc", block, segment[0], preferred_element_type=jnp.float32
        )

    total = product(0, recorded) + product(1, near)
    total = total + product(2, far) + product(3, far_near)
    spectra = total.astype(jnp.bfloat16)[None]
    traces = lax.all_to_all(spectra, FREQ, split_axis=1, concat_axis=0, tiled=True)

    own_y, own_x = lax.axis_index("yl"), lax.axis_index("x")

    def natural(array):
        return with_layout_constraint(array, Layout(major_to_minor=tuple(range(array.ndim))))

    line = line.reshape(rungs, spread, width, pairs, 2, columns)
    stays = lax.dynamic_index_in_dim(line, own_y, axis=1, keepdims=False)
    leaves = lax.dynamic_index_in_dim(line, own_y ^ 1, axis=1, keepdims=False)
    plane = jnp.stack([stays, natural(lax.ppermute(natural(leaves), "yl", [(0, 1), (1, 0)]))])
    pieces = []
    for dx in range(width):
        target = lax.rem(own_x + dx, width)
        piece = natural(lax.dynamic_index_in_dim(plane, target, axis=2, keepdims=False))
        if dx:
            links = [(x, (x + dx) % width) for x in range(width)]
            piece = natural(lax.ppermute(piece, "x", links))
        pieces.append(piece)
    sources = [
        (own_y ^ dy) * width + lax.rem(own_x + width - dx, width)
        for dx in range(width)
        for dy in range(spread)
    ]
    recorded_traces = natural(jnp.stack(pieces).reshape(freq_count, pairs, 2, columns))

    table = lookup_rows(jnp.arange(freq_count) + 1)
    basis = filtered_tables(table, filter_coefficients, tap_delays)

    def station_rows(gathered, s):
        return gathered[:, s].reshape(-1, columns)

    def turned(spectra):
        return with_layout_constraint(spectra.T, Layout(major_to_minor=(0, 1)))

    def to_time(spectra, basis):
        return with_layout_constraint(
            jnp.dot(spectra, basis, preferred_element_type=jnp.float32),
            Layout(major_to_minor=(0, 1)),
        )

    rows = 2 * freq_count
    near_first = jnp.concatenate(
        [
            lax.dynamic_slice_in_dim(table, source * 2 * rungs, 2 * rungs, axis=0)
            for source in sources
        ],
        axis=0,
    )
    data = [
        to_time(turned(station_rows(recorded_traces, s)), near_first).astype(jnp.bfloat16)
        for s in range(2)
    ]

    forward = [(i, i + 1) for i in range(freq_count - 1)]
    backward = [(i + 1, i) for i in range(freq_count - 1)]
    first, second = station_rows(traces, 0), station_rows(traces, 1)
    before = lax.ppermute(second, FREQ, forward)
    after = lax.ppermute(first, FREQ, backward)
    own = turned(jnp.concatenate([first, second], axis=0))
    rest = [
        data[s].astype(jnp.float32) - to_time(own, basis[s, : 2 * rows]) for s in range(2)
    ]
    result = []
    for s, halo in enumerate((before, after)):
        residual = rest[s] - to_time(turned(halo), basis[s, 2 * rows :])
        shrunk = residual - jnp.clip(residual, -shrink_level, shrink_level)
        result.append(shrunk.astype(jnp.bfloat16))
    return jnp.stack(result)


def solution(mesh):
    physical = Mesh(mesh.devices.reshape(SIZES), FREQ + ROW)
    in_specs = (
        P(FREQ, ROW, None, None),
        P(FREQ, ROW, None, None),
        P(None, None, ROW + FREQ),
        P(),
    )
    out_specs = P(ROW + FREQ, None, None)

    return jax.shard_map(
        body, mesh=physical, in_specs=in_specs, out_specs=out_specs, check_vma=False
    )
```

```python
import math

import jax
import jax.numpy as jnp
from jax import lax
from jax.experimental import pallas as pl
from jax.experimental.layout import Layout, with_layout_constraint
from jax.experimental.pallas import tpu as pltpu
from jax.sharding import Mesh
from jax.sharding import PartitionSpec as P


NT = 1024
BLOCK = 128
FREQ = ("yl", "x", "z")
ROW = ("yh", "core")
SIZES = (2, 4, 16, 2, 2)


shrink_level = 0.5


def lookup_rows(frequency_index):
    harmonics = frequency_index.shape[0]
    recording_epochs = jnp.arange(NT)
    rotation_radians = (
        frequency_index[:, None] * recording_epochs[None, :] % NT
    ).astype(jnp.float32) * (2.0 * math.pi / NT)
    scale = 1.0 / math.sqrt(harmonics)
    return jnp.stack(
        [jnp.cos(rotation_radians) * scale, -jnp.sin(rotation_radians) * scale], axis=1
    ).astype(jnp.bfloat16).reshape(2 * harmonics, NT)


def tables_kernel(weights_ref, delays_ref, table_ref, out_ref):
    station = pl.program_id(0)
    rows = table_ref.shape[0]
    taps = delays_ref.shape[0]

    shape = (2 * BLOCK, BLOCK)
    lag = (
        lax.broadcasted_iota(jnp.int32, shape, 1)
        - lax.broadcasted_iota(jnp.int32, shape, 0)
        + BLOCK
    )
    highs, lows = [], []
    for part in range(3):
        neighbour = lax.rem(part + 1 - station, 3)
        band = jnp.zeros(shape, jnp.float32)
        for k in range(taps):
            weight = weights_ref[(neighbour * taps + k) * 2 + station]
            band += jnp.where(lag == delays_ref[k], weight, 0.0)
        highs.append(band.astype(jnp.bfloat16))
        lows.append((band - highs[-1].astype(jnp.float32)).astype(jnp.bfloat16))
    high = jnp.concatenate(highs, axis=1)
    low = jnp.concatenate(lows, axis=1)

    for block in range(NT // BLOCK):
        if block == 0:
            window, skip = table_ref[:, :BLOCK], BLOCK
        else:
            window, skip = table_ref[:, (block - 1) * BLOCK : (block + 1) * BLOCK], 0
        filtered = jnp.dot(window, high[skip:], preferred_element_type=jnp.float32)
        filtered += jnp.dot(window, low[skip:], preferred_element_type=jnp.float32)
        for part in range(3):
            out_ref[0, pl.ds(part * rows, rows), pl.ds(block * BLOCK, BLOCK)] = filtered[
                :, part * BLOCK : (part + 1) * BLOCK
            ].astype(jnp.bfloat16)


def filtered_tables(table, weights, tap_delays):
    rows = table.shape[0]
    return pl.pallas_call(
        tables_kernel,
        grid=(2,),
        out_shape=jax.ShapeDtypeStruct((2, 3 * rows, NT), jnp.bfloat16),
        in_specs=[
            pl.BlockSpec(memory_space=pltpu.SMEM),
            pl.BlockSpec(memory_space=pltpu.SMEM),
            pl.BlockSpec((rows, NT), lambda s: (0, 0)),
        ],
        out_specs=pl.BlockSpec((1, 3 * rows, NT), lambda s: (s, 0, 0)),
        cost_estimate=pl.CostEstimate(
            flops=48 * rows * NT * BLOCK, bytes_accessed=16 * rows * NT, transcendentals=0
        ),
        name="tables",
    )(weights.reshape(-1), tap_delays, table)


def body(operator, recorded, filter_coefficients, tap_delays):
    local_rows = operator.shape[1]
    columns = recorded.shape[3]
    freq_count = lax.axis_size(FREQ)
    row_count = lax.axis_size(ROW)
    row = lax.axis_index(ROW)

    plain = Layout(major_to_minor=(0, 1, 2, 3))

    def across(value, mask):
        pairs = [(i, i ^ mask) for i in range(row_count)]
        return with_layout_constraint(lax.ppermute(value, ROW, pairs), plain)

    spread, width, rungs = (lax.axis_size(axis) for axis in FREQ)
    spots = spread * width
    pairs = local_rows // freq_count

    by_target = recorded.reshape(spots, rungs, pairs, 2, columns).transpose(1, 0, 2, 3, 4)
    line = lax.all_to_all(by_target, "z", split_axis=0, concat_axis=0, tiled=True)

    far = across(recorded, 2)
    near = across(recorded, 1)
    far_near = across(far, 1)

    planes = lax.optimization_barrier(operator[0].transpose(1, 0, 2))

    def product(mask, segment):
        real_part, imag_part = lax.dynamic_slice_in_dim(
            planes, (row ^ mask) * local_rows, local_rows, axis=2
        )
        block = jnp.stack(
            [jnp.stack([real_part, -imag_part]), jnp.stack([imag_part, real_part])]
        )
        return jnp.einsum(
            "qprs,spc->rqc", block, segment[0], preferred_element_type=jnp.float32
        )

    total = product(0, recorded) + product(1, near)
    total = total + product(2, far) + product(3, far_near)
    spectra = total.astype(jnp.bfloat16)[None]
    traces = lax.all_to_all(spectra, FREQ, split_axis=1, concat_axis=0, tiled=True)

    own_y, own_x = lax.axis_index("yl"), lax.axis_index("x")

    def natural(array):
        return with_layout_constraint(array, Layout(major_to_minor=tuple(range(array.ndim))))

    line = line.reshape(rungs, spread, width, pairs, 2, columns)
    stays = lax.dynamic_index_in_dim(line, own_y, axis=1, keepdims=False)
    leaves = lax.dynamic_index_in_dim(line, own_y ^ 1, axis=1, keepdims=False)
    plane = jnp.stack([stays, natural(lax.ppermute(natural(leaves), "yl", [(0, 1), (1, 0)]))])
    pieces = []
    for dx in range(width):
        target = lax.rem(own_x + dx, width)
        piece = natural(lax.dynamic_index_in_dim(plane, target, axis=2, keepdims=False))
        if dx:
            links = [(x, (x + dx) % width) for x in range(width)]
            piece = natural(lax.ppermute(piece, "x", links))
        pieces.append(piece)
    sources = [
        (own_y ^ dy) * width + lax.rem(own_x + width - dx, width)
        for dx in range(width)
        for dy in range(spread)
    ]
    recorded_traces = natural(jnp.stack(pieces).reshape(freq_count, pairs, 2, columns))

    table = lookup_rows(jnp.arange(freq_count) + 1)
    basis = filtered_tables(table, filter_coefficients, tap_delays)

    def station_rows(gathered, s):
        return gathered[:, s].reshape(-1, columns)

    def turned(spectra):
        return with_layout_constraint(spectra.T, Layout(major_to_minor=(0, 1)))

    def to_time(spectra, basis):
        return with_layout_constraint(
            jnp.dot(spectra, basis, preferred_element_type=jnp.float32),
            Layout(major_to_minor=(0, 1)),
        )

    rows = 2 * freq_count
    near_first = jnp.concatenate(
        [
            lax.dynamic_slice_in_dim(table, source * 2 * rungs, 2 * rungs, axis=0)
            for source in sources
        ],
        axis=0,
    )
    data = [
        to_time(turned(station_rows(recorded_traces, s)), near_first).astype(jnp.bfloat16)
        for s in range(2)
    ]

    forward = [(i, i + 1) for i in range(freq_count - 1)]
    backward = [(i + 1, i) for i in range(freq_count - 1)]
    first, second = station_rows(traces, 0), station_rows(traces, 1)
    before = lax.ppermute(second, FREQ, forward)
    after = lax.ppermute(first, FREQ, backward)
    own = turned(jnp.concatenate([first, second], axis=0))
    rest = [
        data[s].astype(jnp.float32) - to_time(own, basis[s, : 2 * rows]) for s in range(2)
    ]
    result = []
    for s, halo in enumerate((before, after)):
        residual = rest[s] - to_time(turned(halo), basis[s, 2 * rows :])
        shrunk = residual - jnp.clip(residual, -shrink_level, shrink_level)
        result.append(shrunk.astype(jnp.bfloat16))
    return jnp.stack(result)


def solution(mesh):
    physical = Mesh(mesh.devices.reshape(SIZES), FREQ + ROW)
    in_specs = (
        P(FREQ, ROW, None, None),
        P(FREQ, ROW, None, None),
        P(None, None, ROW + FREQ),
        P(),
    )
    out_specs = P(ROW + FREQ, None, None)

    return jax.shard_map(
        body, mesh=physical, in_specs=in_specs, out_specs=out_specs, check_vma=False
    )
```

```python
import math

import jax
import jax.numpy as jnp
from jax import lax
from jax.experimental import pallas as pl
from jax.experimental.layout import Layout, with_layout_constraint
from jax.experimental.pallas import tpu as pltpu
from jax.sharding import Mesh
from jax.sharding import PartitionSpec as P


NT = 1024
BLOCK = 128
FREQ = ("yl", "x", "z")
ROW = ("yh", "core")
SIZES = (2, 4, 16, 2, 2)


shrink_level = 0.5


def lookup_rows(frequency_index):
    harmonics = frequency_index.shape[0]
    recording_epochs = jnp.arange(NT)
    rotation_radians = (
        frequency_index[:, None] * recording_epochs[None, :] % NT
    ).astype(jnp.float32) * (2.0 * math.pi / NT)
    scale = 1.0 / math.sqrt(harmonics)
    return jnp.stack(
        [jnp.cos(rotation_radians) * scale, -jnp.sin(rotation_radians) * scale], axis=1
    ).astype(jnp.bfloat16).reshape(2 * harmonics, NT)


def tables_kernel(weights_ref, delays_ref, table_ref, out_ref):
    station = pl.program_id(0)
    rows = table_ref.shape[0]
    taps = delays_ref.shape[0]

    shape = (2 * BLOCK, BLOCK)
    lag = (
        lax.broadcasted_iota(jnp.int32, shape, 1)
        - lax.broadcasted_iota(jnp.int32, shape, 0)
        + BLOCK
    )
    highs, lows = [], []
    for part in range(3):
        neighbour = lax.rem(part + 1 - station, 3)
        band = jnp.zeros(shape, jnp.float32)
        for k in range(taps):
            weight = weights_ref[(neighbour * taps + k) * 2 + station]
            band += jnp.where(lag == delays_ref[k], weight, 0.0)
        highs.append(band.astype(jnp.bfloat16))
        lows.append((band - highs[-1].astype(jnp.float32)).astype(jnp.bfloat16))
    high = jnp.concatenate(highs, axis=1)
    low = jnp.concatenate(lows, axis=1)

    for block in range(NT // BLOCK):
        if block == 0:
            window, skip = table_ref[:, :BLOCK], BLOCK
        else:
            window, skip = table_ref[:, (block - 1) * BLOCK : (block + 1) * BLOCK], 0
        filtered = jnp.dot(window, high[skip:], preferred_element_type=jnp.float32)
        filtered += jnp.dot(window, low[skip:], preferred_element_type=jnp.float32)
        for part in range(3):
            out_ref[0, pl.ds(part * rows, rows), pl.ds(block * BLOCK, BLOCK)] = filtered[
                :, part * BLOCK : (part + 1) * BLOCK
            ].astype(jnp.bfloat16)


def filtered_tables(table, weights, tap_delays):
    rows = table.shape[0]
    return pl.pallas_call(
        tables_kernel,
        grid=(2,),
        out_shape=jax.ShapeDtypeStruct((2, 3 * rows, NT), jnp.bfloat16),
        in_specs=[
            pl.BlockSpec(memory_space=pltpu.SMEM),
            pl.BlockSpec(memory_space=pltpu.SMEM),
            pl.BlockSpec((rows, NT), lambda s: (0, 0)),
        ],
        out_specs=pl.BlockSpec((1, 3 * rows, NT), lambda s: (s, 0, 0)),
        cost_estimate=pl.CostEstimate(
            flops=48 * rows * NT * BLOCK, bytes_accessed=16 * rows * NT, transcendentals=0
        ),
        name="tables",
    )(weights.reshape(-1), tap_delays, table)


def body(operator, recorded, filter_coefficients, tap_delays):
    local_rows = operator.shape[1]
    columns = recorded.shape[3]
    freq_count = lax.axis_size(FREQ)
    row_count = lax.axis_size(ROW)
    row = lax.axis_index(ROW)

    plain = Layout(major_to_minor=(0, 1, 2, 3))

    def across(value, mask):
        pairs = [(i, i ^ mask) for i in range(row_count)]
        return with_layout_constraint(lax.ppermute(value, ROW, pairs), plain)

    spread, width, rungs = (lax.axis_size(axis) for axis in FREQ)
    spots = spread * width
    pairs = local_rows // freq_count

    by_target = recorded.reshape(spots, rungs, pairs, 2, columns).transpose(1, 0, 2, 3, 4)
    line = lax.all_to_all(by_target, "z", split_axis=0, concat_axis=0, tiled=True)

    far = across(recorded, 2)
    near = across(recorded, 1)
    far_near = across(far, 1)

    planes = lax.optimization_barrier(operator[0].transpose(1, 0, 2))

    def product(mask, segment):
        real_part, imag_part = lax.dynamic_slice_in_dim(
            planes, (row ^ mask) * local_rows, local_rows, axis=2
        )
        block = jnp.stack(
            [jnp.stack([real_part, -imag_part]), jnp.stack([imag_part, real_part])]
        )
        return jnp.einsum(
            "qprs,spc->rqc", block, segment[0], preferred_element_type=jnp.float32
        )

    total = product(0, recorded) + product(1, near)
    total = total + product(2, far) + product(3, far_near)
    spectra = total.astype(jnp.bfloat16)[None]
    traces = lax.all_to_all(spectra, FREQ, split_axis=1, concat_axis=0, tiled=True)

    own_y, own_x = lax.axis_index("yl"), lax.axis_index("x")

    def natural(array):
        return with_layout_constraint(array, Layout(major_to_minor=tuple(range(array.ndim))))

    line = line.reshape(rungs, spread, width, pairs, 2, columns)
    stays = lax.dynamic_index_in_dim(line, own_y, axis=1, keepdims=False)
    leaves = lax.dynamic_index_in_dim(line, own_y ^ 1, axis=1, keepdims=False)
    plane = jnp.stack([stays, natural(lax.ppermute(natural(leaves), "yl", [(0, 1), (1, 0)]))])
    pieces = []
    for dx in range(width):
        target = lax.rem(own_x + dx, width)
        piece = natural(lax.dynamic_index_in_dim(plane, target, axis=2, keepdims=False))
        if dx:
            links = [(x, (x + dx) % width) for x in range(width)]
            piece = natural(lax.ppermute(piece, "x", links))
        pieces.append(piece)
    sources = [
        (own_y ^ dy) * width + lax.rem(own_x + width - dx, width)
        for dx in range(width)
        for dy in range(spread)
    ]
    recorded_traces = natural(jnp.stack(pieces).reshape(freq_count, pairs, 2, columns))

    table = lookup_rows(jnp.arange(freq_count) + 1)
    basis = filtered_tables(table, filter_coefficients, tap_delays)

    def station_rows(gathered, s):
        return gathered[:, s].reshape(-1, columns)

    def turned(spectra):
        return with_layout_constraint(spectra.T, Layout(major_to_minor=(0, 1)))

    def to_time(spectra, basis):
        return with_layout_constraint(
            jnp.dot(spectra, basis, preferred_element_type=jnp.float32),
            Layout(major_to_minor=(0, 1)),
        )

    rows = 2 * freq_count
    near_first = jnp.concatenate(
        [
            lax.dynamic_slice_in_dim(table, source * 2 * rungs, 2 * rungs, axis=0)
            for source in sources
        ],
        axis=0,
    )
    data = [
        to_time(turned(station_rows(recorded_traces, s)), near_first).astype(jnp.bfloat16)
        for s in range(2)
    ]

    forward = [(i, i + 1) for i in range(freq_count - 1)]
    backward = [(i + 1, i) for i in range(freq_count - 1)]
    first, second = station_rows(traces, 0), station_rows(traces, 1)
    before = lax.ppermute(second, FREQ, forward)
    after = lax.ppermute(first, FREQ, backward)
    own = turned(jnp.concatenate([first, second], axis=0))
    rest = [
        data[s].astype(jnp.float32) - to_time(own, basis[s, : 2 * rows]) for s in range(2)
    ]
    result = lax.optimization_barrier(jnp.zeros((2, columns, NT), jnp.bfloat16))
    for s, halo in enumerate((before, after)):
        residual = rest[s] - to_time(turned(halo), basis[s, 2 * rows :])
        shrunk = residual - jnp.clip(residual, -shrink_level, shrink_level)
        result = lax.dynamic_update_index_in_dim(
            result, shrunk.astype(jnp.bfloat16), s, axis=0
        )
    return result


def solution(mesh):
    physical = Mesh(mesh.devices.reshape(SIZES), FREQ + ROW)
    in_specs = (
        P(FREQ, ROW, None, None),
        P(FREQ, ROW, None, None),
        P(None, None, ROW + FREQ),
        P(),
    )
    out_specs = P(ROW + FREQ, None, None)

    return jax.shard_map(
        body, mesh=physical, in_specs=in_specs, out_specs=out_specs, check_vma=False
    )
```
